512 devices in a mesh: row: 16 (over z_lo, core), col: 32 (over x, z_hi, y).
Axes of the slice: x: 4, y: 4, z: 16 (z_hi: 2, z_lo: 8; z = z_hi * 8 + z_lo), core: 2. Of those that a mesh axis runs over, the one named last changes fastest.
Arguments:
- inputs: bfloat16 [2048, 12288], P('col', 'row'), may hold values from -6 to 6
- weight: bfloat16 [12288, 24576], P('row', 'col'), may hold values from -0.0546875 to 0.0546875
- grad_out: bfloat16 [2048, 24576], P('row', 'col'), may hold values from -0.890625 to 0.890625
Outputs:
- grad_input: bfloat16 [2048, 12288], P('col', 'row')
- grad_weight: bfloat16 [12288, 24576], P('row', 'col')
The draws below stay inside these ranges and needn't reach their ends.
All inputs are finite; a program needn't handle non-finite values.
Results may differ from the reference program's by a relative error of at most 0.02.
Values may be sent and summed in bfloat16 or wider, within the bound.
No kernel may reach another device: no remote copies, remote signals or barrier semaphores. Data moves between devices by JAX's collectives and lax.ppermute only.
A program may use at most 64 MiB of HBM per device.

```python
import jax
import jax.numpy as jnp
from jax import lax

D = 12288
F = 24576
TOKENS = 2048
N_ROW = 16
N_COL = 32


def block_scale(own_key, extent, shards, least, high):
    level, own = 1.0, jax.random.fold_in(own_key, 6)
    for dim, shards_of in shards:
        draws = jnp.exp(jax.random.uniform(jax.random.fold_in(own, dim), (shards_of,), jnp.float32, least / len(shards), high / len(shards)))
        level = level * jnp.repeat(draws, extent[dim] // shards_of).reshape([-1 if axis == dim else 1 for axis in range(len(extent))])
    return level


def gaussian(rng, dims, width, limit, pieces=(), kind=jnp.bfloat16):
    level = block_scale(rng, dims, pieces, -0.22, 0.18) if pieces else 1.0
    array = jax.random.normal(rng, dims, jnp.float32) * width * level
    return jnp.minimum(jnp.maximum(array, -limit), limit).astype(kind)


def setup_inputs(seed: int = 0) -> dict:
    seeds = jax.random.split(jax.random.key(seed), 4)
    inputs = gaussian(seeds[0], (TOKENS, D), 1.0, 6.0, ((0, 32), (1, 16)))
    weight = gaussian(seeds[1], (D, F), D ** -0.5, 0.0546875, ((0, 16), (1, 32)))
    grad_out = gaussian(seeds[2], (TOKENS, F), (TOKENS ** -0.25), 0.890625, ((0, 16), (1, 32)))
    return {"inputs": inputs, "weight": weight, "grad_out": grad_out}


def gelu_slope(value):
    coef = 0.7978845608
    inner = coef * (value + 0.044715 * value * value * value)
    tanh_val = jnp.tanh(inner)
    return 0.5 * (1.0 + tanh_val) + 0.5 * value * (1.0 - tanh_val * tanh_val) * coef * (1.0 + 3.0 * 0.044715 * value * value)


def reference(inputs, weight, grad_out):
    width_block = D // N_ROW
    unit_block = F // N_COL
    pre = jnp.zeros((inputs.shape[0], weight.shape[1]), jnp.float32)
    for block in range(N_ROW):
        left = inputs[:, block * width_block:(block + 1) * width_block]
        right = weight[block * width_block:(block + 1) * width_block, :]
        partial_sum = jnp.dot(left, right, preferred_element_type=jnp.float32).astype(jnp.bfloat16)
        partial_sum = lax.optimization_barrier(partial_sum)
        pre = pre + partial_sum.astype(jnp.float32)
    grad_pre = (grad_out.astype(jnp.float32) * gelu_slope(pre)).astype(jnp.bfloat16)
    grad_weight = lax.dot_general(inputs, grad_pre, (((0,), (0,)), ((), ())), preferred_element_type=jnp.float32).astype(jnp.bfloat16)
    grad_input = jnp.zeros(inputs.shape, jnp.float32)
    for block in range(N_COL):
        left = grad_pre[:, block * unit_block:(block + 1) * unit_block]
        right = weight[:, block * unit_block:(block + 1) * unit_block]
        term = lax.dot_general(left, right, (((1,), (1,)), ((), ())), preferred_element_type=jnp.float32).astype(jnp.bfloat16)
        term = lax.optimization_barrier(term)
        grad_input = grad_input + term.astype(jnp.float32)
    return grad_input.astype(jnp.bfloat16), grad_weight
```

```python
import jax
import jax.numpy as jnp
from jax import lax
from jax.sharding import Mesh
from jax.sharding import PartitionSpec as P

COL = ("x", "zh", "y")
ROW = ("zl", "core")
XY = ("x", "y")
BF16, F32 = jnp.bfloat16, jnp.float32


def swapped(a, axis):
    return lax.ppermute(a, axis, [(0, 1), (1, 0)])


def up(a, first, last):
    return lax.ppermute(a, "zl", [(j, j + 1) for j in range(first, last)])


def down(a, first, last):
    return lax.ppermute(a, "zl", [(j + 1, j) for j in range(first, last)])


def gelu_slope(value):
    coef = 0.7978845608
    inner = coef * (value + 0.044715 * value * value * value)
    tanh_val = jnp.tanh(inner)
    return 0.5 * (1.0 + tanh_val) + 0.5 * value * (1.0 - tanh_val * tanh_val) * coef * (
        1.0 + 3.0 * 0.044715 * value * value
    )


def block(a, k, axis=0):
    return lax.dynamic_index_in_dim(a, k, axis, keepdims=False)


def to_all(a, n):
    return lax.all_to_all(jnp.broadcast_to(a[None], (n, *a.shape)), XY, 0, 0, tiled=True)


def cotangents(grad_out):
    zl, core = lax.axis_index("zl"), lax.axis_index("core")
    pairs = grad_out.reshape(2, -1, grad_out.shape[-1])
    got = []
    for flip in range(2):
        perm = []
        for src in range(lax.axis_size("zl") * 2):
            pair, a, b = src // 4, src // 2 % 2, src % 2
            perm.append((src, pair * 4 + b * 2 + (a ^ flip)))
        got.append(lax.ppermute(block(pairs, (zl % 2) ^ flip), ROW, perm))
    first = (lax.axis_index("zh") ^ core) == 0
    return jnp.where(first, got[0], got[1]), jnp.where(first, got[1], got[0])


def reduced_rows(parts):
    n = parts.shape[0]
    zl, core = lax.axis_index("zl"), lax.axis_index("core")
    other = swapped(block(parts, 1 - core, 1), "core")
    mine = (block(parts, core, 1).astype(F32) + other.astype(F32)).astype(BF16)
    right = left = None
    for s in range(1, n):
        r, l = block(mine, (zl + n - s) % n), block(mine, (zl + s) % n)
        if right is not None:
            r = (r.astype(F32) + right.astype(F32)).astype(BF16)
            l = (l.astype(F32) + left.astype(F32)).astype(BF16)
        r, l = lax.optimization_barrier((r, l))
        right, left = up(r, 0, s), down(l, n - 1 - s, n - 1)
    return block(mine, zl).astype(F32) + right.astype(F32) + left.astype(F32)


def gathered_rows(own, n):
    zl, core = lax.axis_index("zl"), lax.axis_index("core")
    right, left = [own], [own]
    for k in range(1, n):
        r, l = lax.optimization_barrier((right[-1], left[-1]))
        right.append(up(r, k - 1, n - 1))
        left.append(down(l, 0, n - k))
    line = jnp.zeros((n, *own.shape), own.dtype)
    line = lax.dynamic_update_index_in_dim(line, own, zl, 0)
    for k in range(1, n):
        got = jnp.where(zl >= k, right[k], left[n - k])
        line = lax.dynamic_update_index_in_dim(line, got, (zl - k) % n, 0)
    other = swapped(line, "core")
    low = core == 0
    return jnp.stack([jnp.where(low, line, other), jnp.where(low, other, line)], 1)


def shards(inputs, weight, grad_out):
    n_line = lax.axis_size("zl")
    n_plane = lax.axis_size("x") * lax.axis_size("y")
    tokens, width = inputs.shape
    units = weight.shape[1]
    cots = cotangents(grad_out)
    halves = [to_all(inputs, n_plane), to_all(swapped(inputs, "zh"), n_plane)]
    grads = []
    for half, cot in zip(halves, cots):
        flat = half.reshape(-1, width)
        part = jnp.dot(flat, weight, preferred_element_type=F32).astype(BF16)
        pre = reduced_rows(part.reshape(n_line, 2, tokens, units))
        own = (cot.astype(F32) * gelu_slope(pre)).astype(BF16)
        grads.append(gathered_rows(own, n_line).reshape(-1, units))
    sums = []
    for grad in (grads[1], grads[0]):
        term = lax.dot_general(grad, weight, (((1,), (1,)), ((), ())), preferred_element_type=F32)
        term = term.astype(BF16).reshape(n_plane, tokens, width)
        term = lax.all_to_all(term, XY, 0, 0, tiled=True)
        sums.append(term.astype(F32).sum(0))
    theirs = swapped(sums[0].astype(BF16), "zh")
    grad_input = (sums[1] + theirs.astype(F32)).astype(BF16)
    grad_weight = sum(
        lax.dot_general(
            half.reshape(-1, width), grad, (((0,), (0,)), ((), ())), preferred_element_type=F32
        )
        for half, grad in zip(halves, grads)
    )
    return grad_input, grad_weight.astype(BF16)


def solution(mesh):
    torus = Mesh(mesh.devices.reshape(8, 2, 4, 2, 4), (*ROW, *COL))
    return jax.shard_map(
        shards,
        mesh=torus,
        in_specs=(P(COL, ROW), P(ROW, COL), P(ROW, COL)),
        out_specs=(P(COL, ROW), P(ROW, COL)),
        check_vma=False,
    )
```

```python
import jax
import jax.numpy as jnp
from jax import lax
from jax.sharding import Mesh
from jax.sharding import PartitionSpec as P

COL = ("x", "zh", "y")
ROW = ("zq", "za", "core")
XY = ("x", "y")
BF16, F32 = jnp.bfloat16, jnp.float32


def swapped(a, axis):
    return lax.ppermute(a, axis, [(0, 1), (1, 0)])


def gelu_slope(value):
    coef = 0.7978845608
    inner = coef * (value + 0.044715 * value * value * value)
    tanh_val = jnp.tanh(inner)
    return 0.5 * (1.0 + tanh_val) + 0.5 * value * (1.0 - tanh_val * tanh_val) * coef * (
        1.0 + 3.0 * 0.044715 * value * value
    )


def block(a, k, axis=0):
    return lax.dynamic_index_in_dim(a, k, axis, keepdims=False)


def to_all(a, n):
    return lax.all_to_all(jnp.broadcast_to(a[None], (n, *a.shape)), XY, 0, 0, tiled=True)


def cotangents(grad_out):
    za, core = lax.axis_index("za"), lax.axis_index("core")
    pairs = grad_out.reshape(2, -1, grad_out.shape[-1])
    got = []
    for flip in range(2):
        perm = []
        for src in range(lax.axis_size("zq") * 4):
            quad, a, b = src // 4, src // 2 % 2, src % 2
            perm.append((src, quad * 4 + b * 2 + (a ^ flip)))
        got.append(lax.ppermute(block(pairs, za ^ flip), ROW, perm))
    first = (lax.axis_index("zh") ^ core) == 0
    return jnp.where(first, got[0], got[1]), jnp.where(first, got[1], got[0])


def halved(parts, axis):
    place = lax.axis_index(axis)
    other = swapped(block(parts, 1 - place, 1), axis)
    return (block(parts, place, 1).astype(F32) + other.astype(F32)).astype(BF16)


def doubled(own, axis):
    other = swapped(own, axis)
    low = lax.axis_index(axis) == 0
    return jnp.stack([jnp.where(low, own, other), jnp.where(low, other, own)], 1)


def reduced_rows(parts, tokens, units):
    quads = lax.axis_size("zq")
    parts = halved(parts.reshape(quads * 2, 2, tokens, units), "core")
    parts = halved(parts.reshape(quads, 2, tokens, units), "za")
    return lax.all_to_all(parts, "zq", 0, 0, tiled=True).astype(F32).sum(0)


def gathered_rows(own):
    quads = lax.axis_size("zq")
    line = jnp.broadcast_to(own[None], (quads, *own.shape))
    line = lax.all_to_all(line, "zq", 0, 0, tiled=True)
    line = doubled(line, "za").reshape(quads * 2, *own.shape)
    return doubled(line, "core").reshape(-1, own.shape[-1])


def shards(inputs, weight, grad_out):
    n_plane = lax.axis_size("x") * lax.axis_size("y")
    tokens, width = inputs.shape
    units = weight.shape[1]
    cots = cotangents(grad_out)
    halves = [to_all(inputs, n_plane), to_all(swapped(inputs, "zh"), n_plane)]
    grads = []
    for half, cot in zip(halves, cots):
        flat = half.reshape(-1, width)
        part = jnp.dot(flat, weight, preferred_element_type=F32).astype(BF16)
        pre = reduced_rows(part, tokens, units)
        own = (cot.astype(F32) * gelu_slope(pre)).astype(BF16)
        grads.append(gathered_rows(own))
    sums = []
    for grad in (grads[1], grads[0]):
        term = lax.dot_general(grad, weight, (((1,), (1,)), ((), ())), preferred_element_type=F32)
        term = term.astype(BF16).reshape(n_plane, tokens, width)
        term = lax.all_to_all(term, XY, 0, 0, tiled=True)
        sums.append(term.astype(F32).sum(0))
    theirs = swapped(sums[0].astype(BF16), "zh")
    grad_input = (sums[1] + theirs.astype(F32)).astype(BF16)
    grad_weight = sum(
        lax.dot_general(
            half.reshape(-1, width), grad, (((0,), (0,)), ((), ())), preferred_element_type=F32
        )
        for half, grad in zip(halves, grads)
    )
    return grad_input, grad_weight.astype(BF16)


def solution(mesh):
    torus = Mesh(mesh.devices.reshape(4, 2, 2, 4, 2, 4), (*ROW, *COL))
    return jax.shard_map(
        shards,
        mesh=torus,
        in_specs=(P(COL, ROW), P(ROW, COL), P(ROW, COL)),
        out_specs=(P(COL, ROW), P(ROW, COL)),
        check_vma=False,
    )
```
